32 devices in a mesh: ctx: 8 (over y, x, core), head: 4 (over z).
Axes of the slice: x: 2, y: 2, z: 4, core: 2. Of those that a mesh axis runs over, the one named last changes fastest.
Arguments:
- q_nope: bfloat16 [512, 8192], P('ctx', 'head'), may hold values from -0.59765625 to 0.59765625
- q_rope: bfloat16 [512, 4096], P('ctx', 'head'), may hold values from -6 to 6
- w_uk: bfloat16 [64, 128, 512], P('head'), may hold values from -0.5 to 0.5
- w_uv: bfloat16 [64, 512, 128], P('head'), may hold values from -0.25 to 0.25
- w_o: bfloat16 [8192, 7168], P('head'), may hold values from -0.0625 to 0.0625
- latent_cache: bfloat16 [576, 8192], P(None, 'ctx'), may hold values from -36 to 36
- group_start: int32 [1], replicated, may hold values from 2048 to 7680
Outputs:
- attention_out: bfloat16 [512, 7168], P('ctx', 'head')
The draws below stay inside these ranges and needn't reach their ends.
All inputs are finite; a program needn't handle non-finite values.
Results may differ from the reference program's by a relative error of at most 0.02.
Values may be sent and summed in bfloat16 or wider, within the bound.
A program may use at most 128 MiB of HBM per device.

```python
import math
import jax
import jax.numpy as jnp
from jax import lax

D = 7168
HEADS = 64
LATENT = 512
ROPE = 64
NOPE = 128
VDIM = 128
GROUP = 512
CACHE = 8192


def draw_latent_cache(key, part):
    latent_part = jnp.clip(6.0 * jax.random.normal(jax.random.fold_in(key, 821), (LATENT, CACHE), jnp.float32), -36.0, 36.0)
    rope_part = jnp.clip(jax.random.normal(jax.random.fold_in(key, 822), (ROPE, CACHE), jnp.float32), -6.0, 6.0)
    return jnp.concatenate([latent_part, rope_part], axis=0).astype(jnp.bfloat16)


def draw_q_rope(key, part):
    rope_query = jnp.clip(jax.random.normal(jax.random.fold_in(key, 831), (GROUP, HEADS, ROPE), jnp.float32), -6.0, 6.0)
    return rope_query.reshape(GROUP, HEADS * ROPE).astype(jnp.bfloat16)


def shard_levels(own_key, dims, cuts, low, top_value):
    gain, own = 1.0, jax.random.fold_in(own_key, 6)
    for dim, shards_of in cuts:
        draws = jnp.exp(jax.random.uniform(jax.random.fold_in(own, dim), (shards_of,), jnp.float32, low / len(cuts), top_value / len(cuts)))
        gain = gain * jnp.repeat(draws, dims[dim] // shards_of).reshape([-1 if axis == dim else 1 for axis in range(len(dims))])
    return gain


def noise(rng, extent, spread, reach, cuts=(), kind=jnp.bfloat16):
    values = jax.random.normal(rng, extent, jnp.float32) * spread
    if len(cuts) > 0:
        values = shard_levels(rng, extent, cuts, -0.22, 0.18) * values
    return jnp.clip(values, min=-reach, max=reach).astype(kind)


def setup_inputs(seed: int = 0) -> dict:
    arg_keys = jax.random.split(jax.random.key(seed), 8)
    return {
        "q_nope": noise(arg_keys[0], (GROUP, HEADS * NOPE), 0.1, 0.59765625, ((0, 8), (1, 4))),
        "q_rope": draw_q_rope(jax.random.fold_in(arg_keys[7], 71), 0),
        "w_uk": noise(arg_keys[2], (HEADS, NOPE, LATENT), NOPE ** -0.5, 0.5, ((0, 4),)),
        "w_uv": noise(arg_keys[3], (HEADS, LATENT, VDIM), LATENT ** -0.5, 0.25, ((0, 4),)),
        "w_o": noise(arg_keys[4], (HEADS * VDIM, D), (HEADS * VDIM) ** -0.5, 0.0625, ((0, 4),)),
        "latent_cache": draw_latent_cache(jax.random.fold_in(arg_keys[7], 71), 0),
        "group_start": jax.random.randint(arg_keys[6], (1,), CACHE // 4, CACHE - GROUP + 1).astype(jnp.int32),
    }


masked_score = -1.0e30


def score_scale():
    return (NOPE + ROPE) ** -0.5 * (0.1 * math.log(32.0) + 1.0) ** 2


def reference(q_nope, q_rope, w_uk, w_uv, w_o, latent_cache, group_start):
    nope_part = q_nope.reshape(GROUP, HEADS, NOPE).astype(jnp.float32)
    latent_query = jnp.einsum("thn,hnl->thl", nope_part, w_uk.astype(jnp.float32)).astype(jnp.bfloat16)
    queries = jnp.concatenate([latent_query, q_rope.reshape(GROUP, HEADS, ROPE)], axis=2)
    query_position = group_start[0] + jnp.arange(GROUP, dtype=jnp.int32)
    visible = jnp.arange(CACHE, dtype=jnp.int32)[None, :] <= query_position[:, None]
    values_part = latent_cache[:LATENT]

    def one_head(inputs):
        head_query, head_uv = inputs
        scores = jnp.dot(head_query, latent_cache, preferred_element_type=jnp.float32) * score_scale()
        scores = jnp.where(visible, scores, masked_score)
        row_best = jnp.max(scores, axis=1)
        weights = jnp.where(visible, jnp.exp(scores - row_best[:, None]), 0.0)
        totals = jnp.sum(weights, axis=1)
        numerator = lax.dot_general(weights.astype(jnp.bfloat16), values_part, (((1,), (1,)), ((), ())), preferred_element_type=jnp.float32)
        latent_out = numerator / totals[:, None]
        return jnp.dot(latent_out, head_uv.astype(jnp.float32), precision=lax.Precision.HIGHEST)

    per_head = lax.map(one_head, (jnp.transpose(queries, (1, 0, 2)), w_uv))
    head_values = jnp.transpose(per_head, (1, 0, 2)).reshape(GROUP, HEADS * VDIM).astype(jnp.bfloat16)
    return jnp.dot(head_values, w_o, preferred_element_type=jnp.float32).astype(jnp.bfloat16)
```

```python
import functools
import math

import jax
import jax.numpy as jnp
from jax import lax
from jax.experimental import pallas as pl
from jax.experimental.pallas import tpu as pltpu
from jax.sharding import PartitionSpec as P

LATENT = 512
ROPE = 64
NOPE = 128
VDIM = 128
MESH = pl.DeviceIdType.MESH

masked_score = -1e30
floor_score = -1e29


def score_scale():
    return (NOPE + ROPE) ** (-0.5) * (0.1 * math.log(32.0) + 1.0) ** 2


def exponent_scale():
    return score_scale() * math.log2(math.e)


def peer_chip(chip, step, chips):
    if chips & (chips - 1):
        return lax.rem(chip + step, chips) if step >= 0 else chip
    total = 0
    bit = 1
    while bit < chips:
        flip = 1 if step & bit else 0
        total = total + lax.rem(chip // bit + flip, 2) * bit
        bit *= 2
    return total


def kernel(
    devices, heads_axis, tokens, half, slots, columns,
    start_ref, qn_hbm, qr_hbm, uk_hbm, uv_hbm, wo_hbm, cache_hbm, out_ref,
    wo, keys, values, cache, uk, uv, qn, qr, scores, weights, bias,
    hv_send, hv_recv, lse_send, lse_recv, mix, hv, part, parts_sent, down, up,
    loc_sem, wo_sem, cache_sems, q_send, q_recv, hv_send_sem, hv_recv_sem,
    lse_send_sem, lse_recv_sem, down_send, down_recv, up_send, up_recv,
):
    chips = devices // 2
    me = lax.axis_index("ctx")
    row = lax.axis_index("head")
    chip = me // 2
    core = lax.rem(me, 2)
    other = 1 - core
    partner = chip * 2 + other
    wide = half * NOPE
    roped = half * ROPE
    span = 2 * slots
    pair = 2 * tokens
    local = []

    def begin(src, dst, sem):
        copy = pltpu.make_async_copy(src, dst, sem)
        copy.start()
        return copy

    own_cache = begin(cache_hbm, cache.at[core], loc_sem.at[0])
    own_uk = begin(uk_hbm.at[pl.ds(core * half, half)], uk, loc_sem.at[1])
    own_uv = begin(uv_hbm.at[pl.ds(core * half, half)], uv, loc_sem.at[2])

    def half_n(which):
        return qn_hbm.at[:, pl.ds(pl.multiple_of(which * wide, 128), wide)]

    def half_r(which):
        return qr_hbm.at[:, pl.ds(pl.multiple_of(which * roped, 128), roped)]

    own_qn = begin(half_n(core), qn.at[me], loc_sem.at[3])
    own_qr = begin(half_r(core), qr.at[me], loc_sem.at[4])

    barrier = pltpu.get_barrier_semaphore()
    for step in range(1, devices):
        pl.semaphore_signal(
            barrier, inc=1, device_id={"ctx": lax.rem(me + step, devices)}, device_id_type=MESH
        )

    @pl.when(row > 0)
    def _():
        pl.semaphore_signal(barrier, inc=1, device_id={"head": row - 1}, device_id_type=MESH)

    @pl.when(row < heads_axis - 1)
    def _():
        pl.semaphore_signal(barrier, inc=1, device_id={"head": row + 1}, device_id_type=MESH)

    below = (row + heads_axis - 1) // heads_axis
    above = (2 * heads_axis - 2 - row) // heads_axis
    pl.semaphore_wait(barrier, devices - 1 + below + above)

    def remote(src, dst, send, recv, target):
        return pltpu.make_async_remote_copy(
            src_ref=src, dst_ref=dst, send_sem=send, recv_sem=recv,
            device_id=target, device_id_type=MESH,
        )

    cache_out = remote(
        cache_hbm, cache.at[core], cache_sems.at[0], cache_sems.at[1], {"ctx": partner}
    )
    cache_out.start()
    sent = []

    def send_q(step):
        target_chip = peer_chip(chip, step, chips)
        for which in range(2):
            index = step * 2 + which
            target = {"ctx": target_chip * 2 + which}
            mine = step * 2 + core
            for copy in (
                remote(half_n(which), qn.at[me], q_send.at[index, 0], q_recv.at[mine, 0], target),
                remote(half_r(which), qr.at[me], q_send.at[index, 1], q_recv.at[mine, 1], target),
            ):
                copy.start()
                sent.append(copy)

    for step in range(1, min(3, chips)):
        send_q(step)
    for copy in (
        remote(half_n(other), qn.at[me], q_send.at[0, 0], q_recv.at[core, 0], {"ctx": partner}),
        remote(half_r(other), qr.at[me], q_send.at[0, 1], q_recv.at[core, 1], {"ctx": partner}),
    ):
        copy.start()
        sent.append(copy)
    weight_copies = []
    for dest in range(heads_axis):
        weight_copies.append(
            begin(wo_hbm.at[:, dest * columns:(dest + 1) * columns], wo.at[dest], wo_sem.at[dest])
        )

    scale = exponent_scale()
    own_uk.wait()
    own_uv.wait()
    chunk = 256

    def expand(place):
        uk_rows = uk[...].reshape(half * NOPE, LATENT)
        value_rows = [uv[h].T for h in range(half)]
        value_rows = jnp.concatenate(value_rows, axis=0)

        def body(i, carry):
            here = pl.multiple_of(i * chunk, chunk)
            block = cache[place, :, pl.ds(here, chunk)]
            turned = block.T
            spot = pl.ds(pl.multiple_of(place * slots + here, chunk), chunk)
            nope = lax.dot_general(
                turned[:, :LATENT], uk_rows, (((1,), (1,)), ((), ())),
                preferred_element_type=jnp.float32,
            )
            nope = (nope * scale).astype(jnp.bfloat16)
            rope = (turned[:, LATENT:].astype(jnp.float32) * scale).astype(jnp.bfloat16)
            blank = jnp.zeros_like(rope)
            even = jnp.concatenate([rope, blank], axis=1)
            odd = jnp.concatenate([blank, rope], axis=1)
            for h in range(half):
                keys[h, spot, :NOPE] = nope[:, h * NOPE:(h + 1) * NOPE]
                keys[h, spot, NOPE:] = odd if h % 2 else even
            values[:, spot] = jnp.dot(
                value_rows, block[:LATENT], preferred_element_type=jnp.float32
            ).astype(jnp.bfloat16)
            return carry

        lax.fori_loop(0, slots // chunk, body, 0)

    own_cache.wait()
    expand(core)
    remote(
        cache_hbm, cache.at[other], cache_sems.at[0], cache_sems.at[1], {"ctx": partner}
    ).wait_recv()
    expand(other)
    for step in range(3, chips):
        send_q(step)

    order = list(range(1, chips)) + [0]
    lse_send[...] = jnp.zeros_like(lse_send)
    group_start = start_ref[0]
    block_rows = min(512, span)

    for phase in range(chips // 2):
        both = order[2 * phase:2 * phase + 2]
        sources = []
        for step in both:
            source_chip = peer_chip(chip, step, chips)
            for c in range(2):
                sources.append(source_chip * 2 + c)
            if step == 0:
                own_qn.wait()
                own_qr.wait()
                remote(half_n(core), qn.at[partner], q_send.at[0, 0], q_recv.at[other, 0], {"ctx": partner}).wait_recv()
                remote(half_r(core), qr.at[partner], q_send.at[0, 1], q_recv.at[other, 1], {"ctx": partner}).wait_recv()
            else:
                for c in range(2):
                    src = source_chip * 2 + c
                    index = step * 2 + c
                    remote(half_n(core), qn.at[src], q_send.at[index, 0], q_recv.at[index, 0], {"ctx": src}).wait_recv()
                    remote(half_r(core), qr.at[src], q_send.at[index, 1], q_recv.at[index, 1], {"ctx": src}).wait_recv()
        lanes = lax.broadcasted_iota(jnp.int32, (1, 2 * pair), 1)
        token = jnp.zeros((1, 2 * pair), jnp.int32)
        for i, src in enumerate(sources):
            token = jnp.where(lanes // tokens == i, src * tokens + lanes - i * tokens, token)
        position = token + group_start

        def fill(i, carry):
            here = pl.multiple_of(i * chunk, chunk)
            slot = lax.broadcasted_iota(jnp.int32, (chunk, 2 * pair), 0) + (chip * span + here)
            bias[pl.ds(here, chunk), :] = jnp.where(slot <= position, 0.0, masked_score)
            return carry

        lax.fori_loop(0, span // chunk, fill, 0)

        def head_pair(j, carry):
            for parity in range(2):
                h = j * 2 + parity
                n_cols = pl.ds(pl.multiple_of(h * NOPE, NOPE), NOPE)
                r_cols = pl.ds(pl.multiple_of(j * NOPE, NOPE), NOPE)
                query = jnp.concatenate(
                    [
                        jnp.concatenate([qn[src, :, n_cols], qr[src, :, r_cols]], axis=1)
                        for src in sources
                    ],
                    axis=0,
                )
                best = jnp.full((1, 2 * pair), floor_score, jnp.float32)
                for b in range(span // block_rows):
                    rows = slice(b * block_rows, (b + 1) * block_rows)
                    s = lax.dot_general(
                        keys[h, rows, :], query, (((1,), (1,)), ((), ())),
                        preferred_element_type=jnp.float32,
                    ) + bias[rows, :]
                    scores[parity, rows, :] = s
                    best = jnp.maximum(best, jnp.max(s, axis=0, keepdims=True))
                total = jnp.zeros((1, 2 * pair), jnp.float32)
                for b in range(span // block_rows):
                    rows = slice(b * block_rows, (b + 1) * block_rows)
                    p = jnp.exp2(scores[parity, rows, :] - best)
                    total = total + jnp.sum(p, axis=0, keepdims=True)
                    weights[parity, rows, :] = p.astype(jnp.bfloat16)
                v_rows = pl.ds(pl.multiple_of(h * VDIM, VDIM), VDIM)
                o = jnp.dot(values[v_rows, :], weights[parity], preferred_element_type=jnp.float32)
                safe = jnp.maximum(total, 1e-30)
                o = (o / safe).T.astype(jnp.bfloat16)
                lse = best + jnp.log2(safe)
                for i in range(2):
                    hv_send[2 * phase + i, :, n_cols] = o[i * pair:(i + 1) * pair]
                    lse_send[2 * phase + i, pl.ds(h, 1), :] = lse[:, i * pair:(i + 1) * pair]
            return carry

        lax.fori_loop(0, half // 2, head_pair, 0)

        for i, step in enumerate(both):
            slot = 2 * phase + i
            target_chip = peer_chip(chip, step, chips)
            if step == 0:
                data = hv_send.at[slot, pl.ds(pl.multiple_of(other * tokens, tokens), tokens)]
                kept = hv_send.at[slot, pl.ds(pl.multiple_of(core * tokens, tokens), tokens)]
                local.append(begin(kept, hv_recv.at[chip, core], loc_sem.at[5]))
                local.append(begin(lse_send.at[slot], lse_recv.at[chip, core], loc_sem.at[6]))
                out = [
                    remote(data, hv_recv.at[chip, core], hv_send_sem.at[0], hv_recv_sem.at[core], {"ctx": partner}),
                    remote(lse_send.at[slot], lse_recv.at[chip, core], lse_send_sem.at[0], lse_recv_sem.at[core], {"ctx": partner}),
                ]
            else:
                out = []
                for c in range(2):
                    data = hv_send.at[slot, c * tokens:(c + 1) * tokens]
                    target = {"ctx": target_chip * 2 + c}
                    out.append(remote(data, hv_recv.at[chip, core], hv_send_sem.at[step * 2 + c], hv_recv_sem.at[step * 2 + core], target))
                    out.append(remote(lse_send.at[slot], lse_recv.at[chip, core], lse_send_sem.at[step * 2 + c], lse_recv_sem.at[step * 2 + core], target))
            for copy in out:
                copy.start()
                sent.append(copy)

    for copy in local:
        copy.wait()
    for step in order:
        source_chip = peer_chip(chip, step, chips)
        for c in [other] if step == 0 else [0, 1]:
            index = step * 2 + c
            src = {"ctx": source_chip * 2 + c}
            remote(hv_send.at[0, :tokens], hv_recv.at[source_chip, c], hv_send_sem.at[0], hv_recv_sem.at[index], src).wait_recv()
            remote(lse_send.at[0], lse_recv.at[source_chip, c], lse_send_sem.at[0], lse_recv_sem.at[index], src).wait_recv()

    for c in range(2):
        found = [lse_recv[i, c] for i in range(chips)]
        top = functools.reduce(jnp.maximum, found)
        shares = [jnp.exp2(f - top) for f in found]
        whole = functools.reduce(jnp.add, shares)
        for i in range(chips):
            mix[i] = (shares[i] / whole).T
        mine = pl.ds(pl.multiple_of(core * tokens, tokens), tokens)
        share = [mix[i, mine, :] for i in range(chips)]
        for h in range(half):
            cols = slice(h * VDIM, (h + 1) * VDIM)
            total = jnp.zeros((tokens, VDIM), jnp.float32)
            for i in range(chips):
                total = total + hv_recv[i, c, :, cols].astype(jnp.float32) * share[i][:, h:h + 1]
            hv[:, c * half * VDIM + h * VDIM:c * half * VDIM + (h + 1) * VDIM] = total.astype(jnp.bfloat16)

    for copy in weight_copies:
        copy.wait()
    piece = math.gcd(columns, 896)

    def project(dest):
        for b in range(columns // piece):
            cols = slice(b * piece, (b + 1) * piece)
            part[:, cols] = jnp.dot(hv[...], wo[dest, :, cols], preferred_element_type=jnp.float32)

    last = heads_axis - 1

    def down_copy(dest):
        return remote(parts_sent.at[dest], down.at[dest], down_send.at[dest], down_recv.at[dest], {"head": row + 1})

    def up_copy(dest):
        return remote(parts_sent.at[dest], up.at[dest], up_send.at[dest], up_recv.at[dest], {"head": row - 1})

    def down_wait(dest):
        remote(parts_sent.at[dest], down.at[dest], down_send.at[dest], down_recv.at[dest], {"head": row - 1}).wait_recv()

    def up_wait(dest):
        remote(parts_sent.at[dest], up.at[dest], up_send.at[dest], up_recv.at[dest], {"head": row + 1}).wait_recv()

    at_end = row // last

    def make_part(i, carry):
        dest = last - i + at_end * (2 * i - last)
        project(dest)
        parts_sent[dest] = part[...].astype(jnp.bfloat16)

        @pl.when((row == 0) & (dest > 0))
        def _():
            down_copy(dest).start()

        @pl.when((row == last) & (dest < last))
        def _():
            up_copy(dest).start()

        return carry

    lax.fori_loop(0, heads_axis, make_part, 0)

    upper = (2 * row) // heads_axis
    for i in range(heads_axis):
        turn = last - i // 2 if i % 2 == 0 else i // 2
        dest = turn + upper * (last - 2 * turn)

        @pl.when((row < dest) & (row > 0))
        def _():
            down_wait(dest)
            parts_sent[dest] = parts_sent[dest] + down[dest]
            down_copy(dest).start()

        @pl.when((row > dest) & (row < last))
        def _():
            up_wait(dest)
            parts_sent[dest] = parts_sent[dest] + up[dest]
            up_copy(dest).start()

    part[...] = parts_sent[row].astype(jnp.float32)

    @pl.when(row > 0)
    def _():
        down_wait(row)
        part[...] = part[...] + down[row].astype(jnp.float32)

    @pl.when(row < last)
    def _():
        up_wait(row)
        part[...] = part[...] + up[row].astype(jnp.float32)

    out_ref[...] = part[...].astype(jnp.bfloat16)

    for dest in range(heads_axis):
        @pl.when(row < dest)
        def _():
            down_copy(dest).wait_send()

        @pl.when(row > dest)
        def _():
            up_copy(dest).wait_send()

    cache_out.wait_send()
    for copy in sent:
        copy.wait_send()


def on_device(devices, heads_axis, q_nope, q_rope, w_uk, w_uv, w_o, latent_cache, group_start):
    tokens = q_nope.shape[0]
    half = w_uk.shape[0] // 2
    slots = latent_cache.shape[1]
    width = latent_cache.shape[0]
    columns = w_o.shape[1] // heads_axis
    chips = devices // 2
    pair = 2 * tokens
    span = 2 * slots
    stat_rows = max(8, half)
    bf16, f32 = jnp.bfloat16, jnp.float32
    dma = pltpu.SemaphoreType.DMA
    any_space = pl.BlockSpec(memory_space=pl.ANY)
    return pl.pallas_call(
        functools.partial(kernel, devices, heads_axis, tokens, half, slots, columns),
        out_shape=jax.ShapeDtypeStruct((tokens, columns), bf16),
        in_specs=[pl.BlockSpec(memory_space=pltpu.SMEM)] + [any_space] * 6,
        out_specs=pl.BlockSpec(memory_space=pltpu.VMEM),
        scratch_shapes=[
            pltpu.VMEM((heads_axis, w_o.shape[0], columns), bf16),
            pltpu.VMEM((half, span, 2 * NOPE), bf16),
            pltpu.VMEM((half * VDIM, span), bf16),
            pltpu.VMEM((2, width, slots), bf16),
            pltpu.VMEM((half, NOPE, LATENT), bf16),
            pltpu.VMEM((half, LATENT, VDIM), bf16),
            pltpu.VMEM((devices, tokens, half * NOPE), bf16),
            pltpu.VMEM((devices, tokens, half * ROPE), bf16),
            pltpu.VMEM((2, span, 2 * pair), f32),
            pltpu.VMEM((2, span, 2 * pair), bf16),
            pltpu.VMEM((span, 2 * pair), f32),
            pltpu.VMEM((chips, pair, half * VDIM), bf16),
            pltpu.VMEM((chips, 2, tokens, half * VDIM), bf16),
            pltpu.VMEM((chips, stat_rows, pair), f32),
            pltpu.VMEM((chips, 2, stat_rows, pair), f32),
            pltpu.VMEM((chips, pair, stat_rows), f32),
            pltpu.VMEM((tokens, 2 * half * VDIM), bf16),
            pltpu.VMEM((tokens, columns), f32),
            pltpu.VMEM((heads_axis, tokens, columns), bf16),
            pltpu.VMEM((heads_axis, tokens, columns), bf16),
            pltpu.VMEM((heads_axis, tokens, columns), bf16),
            dma((7,)),
            dma((heads_axis,)),
            dma((2,)),
            dma((devices, 2)),
            dma((devices, 2)),
            dma((devices,)),
            dma((devices,)),
            dma((devices,)),
            dma((devices,)),
            dma((heads_axis,)),
            dma((heads_axis,)),
            dma((heads_axis,)),
            dma((heads_axis,)),
        ],
        compiler_params=pltpu.CompilerParams(
            collective_id=0, has_side_effects=True, vmem_limit_bytes=67043328
        ),
    )(group_start, q_nope, q_rope, w_uk, w_uv, w_o, latent_cache)


def solution(mesh):
    placed = (
        P("ctx", "head"),
        P("ctx", "head"),
        P("head", None, None),
        P("head", None, None),
        P("head", None),
        P(None, "ctx"),
        P(),
    )
    return jax.shard_map(
        functools.partial(on_device, mesh.shape["ctx"], mesh.shape["head"]),
        mesh=mesh, in_specs=placed, out_specs=P("ctx", "head"), check_vma=False,
    )
```

```python
import functools
import math

import jax
import jax.numpy as jnp
from jax import lax
from jax.experimental import pallas as pl
from jax.experimental.pallas import tpu as pltpu
from jax.sharding import PartitionSpec as P

LATENT = 512
ROPE = 64
NOPE = 128
VDIM = 128
MESH = pl.DeviceIdType.MESH

masked_score = -1e30
floor_score = -1e29


def score_scale():
    return (NOPE + ROPE) ** (-0.5) * (0.1 * math.log(32.0) + 1.0) ** 2


def exponent_scale():
    return score_scale() * math.log2(math.e)


def peer_chip(chip, step, chips):
    assert chips & (chips - 1) == 0
    total = 0
    bit = 1
    while bit < chips:
        flip = 1 if step & bit else 0
        total = total + lax.rem(chip // bit + flip, 2) * bit
        bit *= 2
    return total


def kernel(
    devices, heads_axis, tokens, half, slots, columns,
    start_ref, qn_hbm, qr_hbm, uk_hbm, uv_hbm, wo_hbm, cache_hbm, out_ref,
    wo, keys, values, cache, uk, uv, qn, qr, scores, weights, bias,
    hv_send, hv_recv, lse_send, lse_recv, mix, hv, part, parts_sent, down, up,
    loc_sem, wo_sem, cache_sems, q_send, q_recv, hv_send_sem, hv_recv_sem,
    lse_send_sem, lse_recv_sem, down_send, down_recv, up_send, up_recv,
):
    chips = devices // 2
    me = lax.axis_index("ctx")
    row = lax.axis_index("head")
    chip = me // 2
    core = lax.rem(me, 2)
    other = 1 - core
    partner = chip * 2 + other
    wide = half * NOPE
    roped = half * ROPE
    span = 2 * slots
    part_rows = tokens // 2
    pair = 2 * part_rows
    lanes_total = devices * part_rows
    local = []

    def begin(src, dst, sem):
        copy = pltpu.make_async_copy(src, dst, sem)
        copy.start()
        return copy

    own_cache = begin(cache_hbm, cache.at[core], loc_sem.at[0])
    own_uk = begin(uk_hbm.at[pl.ds(core * half, half)], uk, loc_sem.at[1])
    own_uv = begin(uv_hbm.at[pl.ds(core * half, half)], uv, loc_sem.at[2])

    def rows_of(phase):
        return pl.ds(phase * part_rows, part_rows)

    def half_n(which, phase):
        return qn_hbm.at[rows_of(phase), pl.ds(pl.multiple_of(which * wide, 128), wide)]

    def half_r(which, phase):
        return qr_hbm.at[rows_of(phase), pl.ds(pl.multiple_of(which * roped, 128), roped)]

    own_q = []
    for phase in range(2):
        own_q.append(begin(half_n(core, phase), qn.at[me, rows_of(phase)], loc_sem.at[3 + 2 * phase]))
        own_q.append(begin(half_r(core, phase), qr.at[me, rows_of(phase)], loc_sem.at[4 + 2 * phase]))

    barrier = pltpu.get_barrier_semaphore()
    for step in range(1, devices):
        pl.semaphore_signal(
            barrier, inc=1, device_id={"ctx": lax.rem(me + step, devices)}, device_id_type=MESH
        )

    @pl.when(row > 0)
    def _():
        pl.semaphore_signal(barrier, inc=1, device_id={"head": row - 1}, device_id_type=MESH)

    @pl.when(row < heads_axis - 1)
    def _():
        pl.semaphore_signal(barrier, inc=1, device_id={"head": row + 1}, device_id_type=MESH)

    below = (row + heads_axis - 1) // heads_axis
    above = (2 * heads_axis - 2 - row) // heads_axis
    pl.semaphore_wait(barrier, devices - 1 + below + above)

    def remote(src, dst, send, recv, target):
        return pltpu.make_async_remote_copy(
            src_ref=src, dst_ref=dst, send_sem=send, recv_sem=recv,
            device_id=target, device_id_type=MESH,
        )

    cache_out = remote(
        cache_hbm, cache.at[core], cache_sems.at[0], cache_sems.at[1], {"ctx": partner}
    )
    cache_out.start()
    sent = []

    def q_copies(phase, source, which, target, index, mine):
        rows = rows_of(phase)
        return (
            remote(half_n(which, phase), qn.at[source, rows], q_send.at[phase, index, 0], q_recv.at[phase, mine, 0], {"ctx": target}),
            remote(half_r(which, phase), qr.at[source, rows], q_send.at[phase, index, 1], q_recv.at[phase, mine, 1], {"ctx": target}),
        )

    def send_q(phase):
        for step in range(1, chips):
            target_chip = peer_chip(chip, step, chips)
            for which in range(2):
                for copy in q_copies(phase, me, which, target_chip * 2 + which, step * 2 + which, step * 2 + core):
                    copy.start()
                    sent.append(copy)
        for copy in q_copies(phase, me, other, partner, 0, core):
            copy.start()
            sent.append(copy)

    send_q(0)
    weight_copies = []
    for dest in range(heads_axis):
        weight_copies.append(
            begin(wo_hbm.at[:, dest * columns:(dest + 1) * columns], wo.at[dest], wo_sem.at[dest])
        )

    scale = exponent_scale()
    own_uk.wait()
    own_uv.wait()
    chunk = 256

    def expand(place):
        uk_rows = uk[...].reshape(half * NOPE, LATENT)
        value_rows = [uv[h].T for h in range(half)]
        value_rows = jnp.concatenate(value_rows, axis=0)

        def body(i, carry):
            here = pl.multiple_of(i * chunk, chunk)
            block = cache[place, :, pl.ds(here, chunk)]
            turned = block.T
            spot = pl.ds(pl.multiple_of(place * slots + here, chunk), chunk)
            nope = lax.dot_general(
                turned[:, :LATENT], uk_rows, (((1,), (1,)), ((), ())),
                preferred_element_type=jnp.float32,
            )
            nope = (nope * scale).astype(jnp.bfloat16)
            rope = (turned[:, LATENT:].astype(jnp.float32) * scale).astype(jnp.bfloat16)
            blank = jnp.zeros_like(rope)
            even = jnp.concatenate([rope, blank], axis=1)
            odd = jnp.concatenate([blank, rope], axis=1)
            for h in range(half):
                keys[h, spot, :NOPE] = nope[:, h * NOPE:(h + 1) * NOPE]
                keys[h, spot, NOPE:] = odd if h % 2 else even
            values[:, spot] = jnp.dot(
                value_rows, block[:LATENT], preferred_element_type=jnp.float32
            ).astype(jnp.bfloat16)
            return carry

        lax.fori_loop(0, slots // chunk, body, 0)

    own_cache.wait()
    expand(core)
    send_q(1)
    remote(
        cache_hbm, cache.at[other], cache_sems.at[0], cache_sems.at[1], {"ctx": partner}
    ).wait_recv()
    expand(other)

    order = list(range(1, chips)) + [0]
    lse_send[...] = jnp.zeros_like(lse_send)
    group_start = start_ref[0]
    block_rows = min(512, span)

    for phase in range(2):
        sources = []
        for step in order:
            source_chip = peer_chip(chip, step, chips)
            for c in range(2):
                sources.append(source_chip * 2 + c)
            if step == 0:
                own_q[2 * phase].wait()
                own_q[2 * phase + 1].wait()
                for copy in q_copies(phase, partner, core, partner, 0, other):
                    copy.wait_recv()
            else:
                for c in range(2):
                    src = source_chip * 2 + c
                    for copy in q_copies(phase, src, core, src, step * 2 + c, step * 2 + c):
                        copy.wait_recv()
        lanes = lax.broadcasted_iota(jnp.int32, (1, lanes_total), 1)
        token = jnp.zeros((1, lanes_total), jnp.int32)
        for i, src in enumerate(sources):
            token = jnp.where(
                lanes // part_rows == i,
                src * tokens + phase * part_rows + lanes - i * part_rows, token,
            )
        position = token + group_start

        def fill(i, carry):
            here = pl.multiple_of(i * chunk, chunk)
            slot = lax.broadcasted_iota(jnp.int32, (chunk, lanes_total), 0) + (chip * span + here)
            bias[pl.ds(here, chunk), :] = jnp.where(slot <= position, 0.0, masked_score)
            return carry

        lax.fori_loop(0, span // chunk, fill, 0)

        token_rows = slice(phase * part_rows, (phase + 1) * part_rows)

        def head_pair(j, carry):
            for parity in range(2):
                h = j * 2 + parity
                n_cols = pl.ds(pl.multiple_of(h * NOPE, NOPE), NOPE)
                r_cols = pl.ds(pl.multiple_of(j * NOPE, NOPE), NOPE)
                query = jnp.concatenate(
                    [
                        jnp.concatenate([qn[src, token_rows, n_cols], qr[src, token_rows, r_cols]], axis=1)
                        for src in sources
                    ],
                    axis=0,
                )
                best = jnp.full((1, lanes_total), floor_score, jnp.float32)
                for b in range(span // block_rows):
                    rows = slice(b * block_rows, (b + 1) * block_rows)
                    s = lax.dot_general(
                        keys[h, rows, :], query, (((1,), (1,)), ((), ())),
                        preferred_element_type=jnp.float32,
                    ) + bias[rows, :]
                    scores[parity, rows, :] = s
                    best = jnp.maximum(best, jnp.max(s, axis=0, keepdims=True))
                total = jnp.zeros((1, lanes_total), jnp.float32)
                for b in range(span // block_rows):
                    rows = slice(b * block_rows, (b + 1) * block_rows)
                    p = jnp.exp2(scores[parity, rows, :] - best)
                    total = total + jnp.sum(p, axis=0, keepdims=True)
                    weights[parity, rows, :] = p.astype(jnp.bfloat16)
                v_rows = pl.ds(pl.multiple_of(h * VDIM, VDIM), VDIM)
                o = jnp.dot(values[v_rows, :], weights[parity], preferred_element_type=jnp.float32)
                safe = jnp.maximum(total, 1e-30)
                o = (o / safe).T.astype(jnp.bfloat16)
                lse = best + jnp.log2(safe)
                for i in range(chips):
                    hv_send[phase, i, :, n_cols] = o[i * pair:(i + 1) * pair]
                for i in range(chips // 2):
                    lse_send[phase, i, pl.ds(h, 1), :] = lse[:, 2 * i * pair:2 * (i + 1) * pair]
            return carry

        lax.fori_loop(0, half // 2, head_pair, 0)

        for i, step in enumerate(order):
            target_chip = peer_chip(chip, step, chips)
            stats = lse_send.at[phase, i // 2]
            for c in range(2):
                if step == 0 and c == 1:
                    continue
                index = step * 2 + c
                if step == 0:
                    data = hv_send.at[phase, i, pl.ds(pl.multiple_of(other * part_rows, part_rows), part_rows)]
                    kept = hv_send.at[phase, i, pl.ds(pl.multiple_of(core * part_rows, part_rows), part_rows)]
                    local.append(begin(kept, hv_recv.at[phase, i, core], loc_sem.at[7 + 2 * phase]))
                    local.append(begin(stats, lse_recv.at[phase, i, core], loc_sem.at[8 + 2 * phase]))
                    target = {"ctx": partner}
                else:
                    data = hv_send.at[phase, i, c * part_rows:(c + 1) * part_rows]
                    target = {"ctx": target_chip * 2 + c}
                mine = step * 2 + core
                for copy in (
                    remote(data, hv_recv.at[phase, i, core], hv_send_sem.at[phase, index], hv_recv_sem.at[phase, mine], target),
                    remote(stats, lse_recv.at[phase, i, core], lse_send_sem.at[phase, index], lse_recv_sem.at[phase, mine], target),
                ):
                    copy.start()
                    sent.append(copy)

    def combine(phase):
        local[2 * phase].wait()
        local[2 * phase + 1].wait()
        for i, step in enumerate(order):
            source_chip = peer_chip(chip, step, chips)
            for c in [other] if step == 0 else [0, 1]:
                index = step * 2 + c
                src = {"ctx": source_chip * 2 + c}
                remote(hv_send.at[phase, 0, :part_rows], hv_recv.at[phase, i, c], hv_send_sem.at[phase, 0], hv_recv_sem.at[phase, index], src).wait_recv()
                remote(lse_send.at[phase, 0], lse_recv.at[phase, i, c], lse_send_sem.at[phase, 0], lse_recv_sem.at[phase, index], src).wait_recv()
        for c in range(2):
            found = []
            for i in range(chips):
                mix[i] = lse_recv[phase, i, c].T
                first = pl.multiple_of((i % 2) * pair + core * part_rows, part_rows)
                found.append(mix[i, pl.ds(first, part_rows), :])
            top = functools.reduce(jnp.maximum, found)
            shares = [jnp.exp2(f - top) for f in found]
            whole = functools.reduce(jnp.add, shares)
            share = [f / whole for f in shares]
            for h in range(half):
                cols = slice(h * VDIM, (h + 1) * VDIM)
                total = jnp.zeros((part_rows, VDIM), jnp.float32)
                for i in range(chips):
                    total = total + hv_recv[phase, i, c, :, cols].astype(jnp.float32) * share[i][:, h:h + 1]
                first = (c * half + h) * VDIM
                hv[:, first:first + VDIM] = total.astype(jnp.bfloat16)

    piece = math.gcd(columns, 896)

    def project(dest):
        for b in range(columns // piece):
            cols = slice(b * piece, (b + 1) * piece)
            part[:, cols] = jnp.dot(hv[...], wo[dest, :, cols], preferred_element_type=jnp.float32)

    last = heads_axis - 1

    def chain(phase, dest, buffer, sends, recvs, target):
        return remote(parts_sent.at[phase, dest], buffer.at[phase, dest], sends.at[phase, dest], recvs.at[phase, dest], {"head": target})

    def down_copy(phase, dest):
        return chain(phase, dest, down, down_send, down_recv, row + 1)

    def up_copy(phase, dest):
        return chain(phase, dest, up, up_send, up_recv, row - 1)

    def down_wait(phase, dest):
        chain(phase, dest, down, down_send, down_recv, row - 1).wait_recv()

    def up_wait(phase, dest):
        chain(phase, dest, up, up_send, up_recv, row + 1).wait_recv()

    at_end = row // last
    upper = (2 * row) // heads_axis

    for phase in range(2):
        combine(phase)
        if phase == 0:
            for copy in weight_copies:
                copy.wait()

        def make_part(i, carry):
            dest = last - i + at_end * (2 * i - last)
            project(dest)
            parts_sent[phase, dest] = part[...].astype(jnp.bfloat16)

            @pl.when((row == 0) & (dest > 0))
            def _():
                down_copy(phase, dest).start()

            @pl.when((row == last) & (dest < last))
            def _():
                up_copy(phase, dest).start()

            return carry

        lax.fori_loop(0, heads_axis, make_part, 0)

        for i in range(heads_axis):
            turn = last - i // 2 if i % 2 == 0 else i // 2
            dest = turn + upper * (last - 2 * turn)

            @pl.when((row < dest) & (row > 0))
            def _():
                down_wait(phase, dest)
                parts_sent[phase, dest] = parts_sent[phase, dest] + down[phase, dest]
                down_copy(phase, dest).start()

            @pl.when((row > dest) & (row < last))
            def _():
                up_wait(phase, dest)
                parts_sent[phase, dest] = parts_sent[phase, dest] + up[phase, dest]
                up_copy(phase, dest).start()

    for phase in range(2):
        part[...] = parts_sent[phase, row].astype(jnp.float32)

        @pl.when(row > 0)
        def _():
            down_wait(phase, row)
            part[...] = part[...] + down[phase, row].astype(jnp.float32)

        @pl.when(row < last)
        def _():
            up_wait(phase, row)
            part[...] = part[...] + up[phase, row].astype(jnp.float32)

        out_ref[phase * part_rows:(phase + 1) * part_rows, :] = part[...].astype(jnp.bfloat16)

    for phase in range(2):
        for dest in range(heads_axis):
            @pl.when(row < dest)
            def _():
                down_copy(phase, dest).wait_send()

            @pl.when(row > dest)
            def _():
                up_copy(phase, dest).wait_send()

    cache_out.wait_send()
    for copy in sent:
        copy.wait_send()


def on_device(devices, heads_axis, q_nope, q_rope, w_uk, w_uv, w_o, latent_cache, group_start):
    tokens = q_nope.shape[0]
    half = w_uk.shape[0] // 2
    slots = latent_cache.shape[1]
    width = latent_cache.shape[0]
    columns = w_o.shape[1] // heads_axis
    chips = devices // 2
    part_rows = tokens // 2
    pair = 2 * part_rows
    lanes_total = devices * part_rows
    span = 2 * slots
    stat_rows = max(8, half)
    bf16, f32 = jnp.bfloat16, jnp.float32
    dma = pltpu.SemaphoreType.DMA
    any_space = pl.BlockSpec(memory_space=pl.ANY)
    return pl.pallas_call(
        functools.partial(kernel, devices, heads_axis, tokens, half, slots, columns),
        out_shape=jax.ShapeDtypeStruct((tokens, columns), bf16),
        in_specs=[pl.BlockSpec(memory_space=pltpu.SMEM)] + [any_space] * 6,
        out_specs=pl.BlockSpec(memory_space=pltpu.VMEM),
        scratch_shapes=[
            pltpu.VMEM((heads_axis, w_o.shape[0], columns), bf16),
            pltpu.VMEM((half, span, 2 * NOPE), bf16),
            pltpu.VMEM((half * VDIM, span), bf16),
            pltpu.VMEM((2, width, slots), bf16),
            pltpu.VMEM((half, NOPE, LATENT), bf16),
            pltpu.VMEM((half, LATENT, VDIM), bf16),
            pltpu.VMEM((devices, tokens, half * NOPE), bf16),
            pltpu.VMEM((devices, tokens, half * ROPE), bf16),
            pltpu.VMEM((2, span, lanes_total), f32),
            pltpu.VMEM((2, span, lanes_total), bf16),
            pltpu.VMEM((span, lanes_total), f32),
            pltpu.VMEM((2, chips, pair, half * VDIM), bf16),
            pltpu.VMEM((2, chips, 2, part_rows, half * VDIM), bf16),
            pltpu.VMEM((2, chips // 2, stat_rows, 2 * pair), f32),
            pltpu.VMEM((2, chips, 2, stat_rows, 2 * pair), f32),
            pltpu.VMEM((chips, 2 * pair, stat_rows), f32),
            pltpu.VMEM((part_rows, 2 * half * VDIM), bf16),
            pltpu.VMEM((part_rows, columns), f32),
            pltpu.VMEM((2, heads_axis, part_rows, columns), bf16),
            pltpu.VMEM((2, heads_axis, part_rows, columns), bf16),
            pltpu.VMEM((2, heads_axis, part_rows, columns), bf16),
            dma((11,)),
            dma((heads_axis,)),
            dma((2,)),
            dma((2, devices, 2)),
            dma((2, devices, 2)),
            dma((2, devices)),
            dma((2, devices)),
            dma((2, devices)),
            dma((2, devices)),
            dma((2, heads_axis)),
            dma((2, heads_axis)),
            dma((2, heads_axis)),
            dma((2, heads_axis)),
        ],
        compiler_params=pltpu.CompilerParams(
            collective_id=0, has_side_effects=True, vmem_limit_bytes=67043328
        ),
    )(group_start, q_nope, q_rope, w_uk, w_uv, w_o, latent_cache)


def solution(mesh):
    placed = (
        P("ctx", "head"),
        P("ctx", "head"),
        P("head", None, None),
        P("head", None, None),
        P("head", None),
        P(None, "ctx"),
        P(),
    )
    return jax.shard_map(
        functools.partial(on_device, mesh.shape["ctx"], mesh.shape["head"]),
        mesh=mesh, in_specs=placed, out_specs=P("ctx", "head"), check_vma=False,
    )
```

```python
import functools
import math

import jax
import jax.numpy as jnp
from jax import lax
from jax.experimental import pallas as pl
from jax.experimental.pallas import tpu as pltpu
from jax.sharding import PartitionSpec as P

LATENT = 512
ROPE = 64
NOPE = 128
VDIM = 128
MESH = pl.DeviceIdType.MESH

masked_score = -1e30
floor_score = -1e29


def score_scale():
    return (NOPE + ROPE) ** (-0.5) * (0.1 * math.log(32.0) + 1.0) ** 2


def exponent_scale():
    return score_scale() * math.log2(math.e)


def peer_chip(chip, step, chips):
    assert chips & (chips - 1) == 0
    total = 0
    bit = 1
    while bit < chips:
        flip = 1 if step & bit else 0
        total = total + lax.rem(chip // bit + flip, 2) * bit
        bit *= 2
    return total


def kernel(
    devices, heads_axis, tokens, half, slots, columns,
    start_ref, qn_hbm, qr_hbm, uk_hbm, uv_hbm, wo_hbm, cache_hbm, out_ref,
    wo, keys, values, cache, uk, uv, qn, qr, scores, weights, bias,
    hv_send, hv_recv, lse_send, lse_recv, mix, hv, part, parts_sent, down, up,
    loc_sem, wo_sem, cache_sems, q_send, q_recv, hv_send_sem, hv_recv_sem,
    lse_send_sem, lse_recv_sem, down_send, down_recv, up_send, up_recv,
):
    chips = devices // 2
    me = lax.axis_index("ctx")
    row = lax.axis_index("head")
    chip = me // 2
    core = lax.rem(me, 2)
    other = 1 - core
    partner = chip * 2 + other
    wide = half * NOPE
    roped = half * ROPE
    span = 2 * slots
    part_rows = tokens // 2
    pair = 2 * part_rows
    lanes_total = devices * part_rows
    local = []

    def begin(src, dst, sem):
        copy = pltpu.make_async_copy(src, dst, sem)
        copy.start()
        return copy

    own_cache = begin(cache_hbm, cache.at[core], loc_sem.at[0])
    own_uk = begin(uk_hbm.at[pl.ds(core * half, half)], uk, loc_sem.at[1])
    own_uv = begin(uv_hbm.at[pl.ds(core * half, half)], uv, loc_sem.at[2])

    def rows_of(phase):
        return pl.ds(phase * part_rows, part_rows)

    def half_n(which, phase):
        return qn_hbm.at[rows_of(phase), pl.ds(pl.multiple_of(which * wide, 128), wide)]

    def half_r(which, phase):
        return qr_hbm.at[rows_of(phase), pl.ds(pl.multiple_of(which * roped, 128), roped)]

    own_q = []
    for phase in range(2):
        own_q.append(begin(half_n(core, phase), qn.at[me, rows_of(phase)], loc_sem.at[3 + 2 * phase]))
        own_q.append(begin(half_r(core, phase), qr.at[me, rows_of(phase)], loc_sem.at[4 + 2 * phase]))

    barrier = pltpu.get_barrier_semaphore()
    for step in range(1, devices):
        pl.semaphore_signal(
            barrier, inc=1, device_id={"ctx": lax.rem(me + step, devices)}, device_id_type=MESH
        )

    @pl.when(row > 0)
    def _():
        pl.semaphore_signal(barrier, inc=1, device_id={"head": row - 1}, device_id_type=MESH)

    @pl.when(row < heads_axis - 1)
    def _():
        pl.semaphore_signal(barrier, inc=1, device_id={"head": row + 1}, device_id_type=MESH)

    below = (row + heads_axis - 1) // heads_axis
    above = (2 * heads_axis - 2 - row) // heads_axis
    pl.semaphore_wait(barrier, devices - 1 + below + above)

    def remote(src, dst, send, recv, target):
        return pltpu.make_async_remote_copy(
            src_ref=src, dst_ref=dst, send_sem=send, recv_sem=recv,
            device_id=target, device_id_type=MESH,
        )

    cache_out = remote(
        cache_hbm, cache.at[core], cache_sems.at[0], cache_sems.at[1], {"ctx": partner}
    )
    cache_out.start()
    sent = []

    def q_copies(phase, source, which, target, index, mine):
        rows = rows_of(phase)
        return (
            remote(half_n(which, phase), qn.at[source, rows], q_send.at[phase, index, 0], q_recv.at[phase, mine, 0], {"ctx": target}),
            remote(half_r(which, phase), qr.at[source, rows], q_send.at[phase, index, 1], q_recv.at[phase, mine, 1], {"ctx": target}),
        )

    def send_q(phase):
        for step in range(1, chips):
            target_chip = peer_chip(chip, step, chips)
            for which in range(2):
                for copy in q_copies(phase, me, which, target_chip * 2 + which, step * 2 + which, step * 2 + core):
                    copy.start()
                    sent.append(copy)
        for copy in q_copies(phase, me, other, partner, 0, core):
            copy.start()
            sent.append(copy)

    send_q(0)
    weight_copies = []
    for dest in range(heads_axis):
        weight_copies.append(
            begin(wo_hbm.at[:, dest * columns:(dest + 1) * columns], wo.at[dest], wo_sem.at[dest])
        )

    scale = exponent_scale()
    own_uk.wait()
    own_uv.wait()
    chunk = 256

    def expand(place):
        uk_rows = uk[...].reshape(half * NOPE, LATENT)
        value_rows = [uv[h].T for h in range(half)]
        value_rows = jnp.concatenate(value_rows, axis=0)

        def body(i, carry):
            here = pl.multiple_of(i * chunk, chunk)
            block = cache[place, :, pl.ds(here, chunk)]
            turned = block.T
            spot = pl.ds(pl.multiple_of(place * slots + here, chunk), chunk)
            nope = lax.dot_general(
                turned[:, :LATENT], uk_rows, (((1,), (1,)), ((), ())),
                preferred_element_type=jnp.float32,
            )
            nope = (nope * scale).astype(jnp.bfloat16)
            rope = (turned[:, LATENT:].astype(jnp.float32) * scale).astype(jnp.bfloat16)
            blank = jnp.zeros_like(rope)
            even = jnp.concatenate([rope, blank], axis=1)
            odd = jnp.concatenate([blank, rope], axis=1)
            for h in range(half):
                keys[h, spot, :NOPE] = nope[:, h * NOPE:(h + 1) * NOPE]
                keys[h, spot, NOPE:] = odd if h % 2 else even
            values[:, spot] = jnp.dot(
                value_rows, block[:LATENT], preferred_element_type=jnp.float32
            ).astype(jnp.bfloat16)
            return carry

        lax.fori_loop(0, slots // chunk, body, 0)

    own_cache.wait()
    expand(core)
    send_q(1)
    remote(
        cache_hbm, cache.at[other], cache_sems.at[0], cache_sems.at[1], {"ctx": partner}
    ).wait_recv()
    expand(other)

    order = list(range(1, chips)) + [0]
    lse_send[...] = jnp.zeros_like(lse_send)
    group_start = start_ref[0]
    block_rows = min(512, span)

    for phase in range(2):
        sources = []
        for step in order:
            source_chip = peer_chip(chip, step, chips)
            for c in range(2):
                sources.append(source_chip * 2 + c)
        lanes = lax.broadcasted_iota(jnp.int32, (1, lanes_total), 1)
        token = jnp.zeros((1, lanes_total), jnp.int32)
        for i, src in enumerate(sources):
            token = jnp.where(
                lanes // part_rows == i,
                src * tokens + phase * part_rows + lanes - i * part_rows, token,
            )
        position = token + group_start

        def fill(i, carry):
            here = pl.multiple_of(i * chunk, chunk)
            slot = lax.broadcasted_iota(jnp.int32, (chunk, lanes_total), 0) + (chip * span + here)
            bias[pl.ds(here, chunk), :] = jnp.where(slot <= position, 0.0, masked_score)
            return carry

        lax.fori_loop(0, span // chunk, fill, 0)

        for step in order:
            source_chip = peer_chip(chip, step, chips)
            if step == 0:
                own_q[2 * phase].wait()
                own_q[2 * phase + 1].wait()
                for copy in q_copies(phase, partner, core, partner, 0, other):
                    copy.wait_recv()
            else:
                for c in range(2):
                    src = source_chip * 2 + c
                    for copy in q_copies(phase, src, core, src, step * 2 + c, step * 2 + c):
                        copy.wait_recv()

        token_rows = slice(phase * part_rows, (phase + 1) * part_rows)

        def head_pair(j, carry):
            for parity in range(2):
                h = j * 2 + parity
                n_cols = pl.ds(pl.multiple_of(h * NOPE, NOPE), NOPE)
                r_cols = pl.ds(pl.multiple_of(j * NOPE, NOPE), NOPE)
                query = jnp.concatenate(
                    [
                        jnp.concatenate([qn[src, token_rows, n_cols], qr[src, token_rows, r_cols]], axis=1)
                        for src in sources
                    ],
                    axis=0,
                )
                best = jnp.full((1, lanes_total), floor_score, jnp.float32)
                for b in range(span // block_rows):
                    rows = slice(b * block_rows, (b + 1) * block_rows)
                    s = lax.dot_general(
                        keys[h, rows, :], query, (((1,), (1,)), ((), ())),
                        preferred_element_type=jnp.float32,
                    ) + bias[rows, :]
                    scores[parity, rows, :] = s
                    best = jnp.maximum(best, jnp.max(s, axis=0, keepdims=True))
                total = jnp.zeros((1, lanes_total), jnp.float32)
                for b in range(span // block_rows):
                    rows = slice(b * block_rows, (b + 1) * block_rows)
                    p = jnp.exp2(scores[parity, rows, :] - best)
                    total = total + jnp.sum(p, axis=0, keepdims=True)
                    weights[parity, rows, :] = p.astype(jnp.bfloat16)
                v_rows = pl.ds(pl.multiple_of(h * VDIM, VDIM), VDIM)
                o = jnp.dot(values[v_rows, :], weights[parity], preferred_element_type=jnp.float32)
                safe = jnp.maximum(total, 1e-30)
                o = (o / safe).T.astype(jnp.bfloat16)
                lse = best + jnp.log2(safe)
                for i in range(chips):
                    hv_send[phase, i, :, n_cols] = o[i * pair:(i + 1) * pair]
                for i in range(chips // 2):
                    lse_send[phase, i, pl.ds(h, 1), :] = lse[:, 2 * i * pair:2 * (i + 1) * pair]
            return carry

        lax.fori_loop(0, half // 2, head_pair, 0, unroll=2)

        for i, step in enumerate(order):
            target_chip = peer_chip(chip, step, chips)
            stats = lse_send.at[phase, i // 2]
            for c in range(2):
                if step == 0 and c == 1:
                    continue
                index = step * 2 + c
                if step == 0:
                    data = hv_send.at[phase, i, pl.ds(pl.multiple_of(other * part_rows, part_rows), part_rows)]
                    kept = hv_send.at[phase, i, pl.ds(pl.multiple_of(core * part_rows, part_rows), part_rows)]
                    local.append(begin(kept, hv_recv.at[phase, i, core], loc_sem.at[7 + 2 * phase]))
                    local.append(begin(stats, lse_recv.at[phase, i, core], loc_sem.at[8 + 2 * phase]))
                    target = {"ctx": partner}
                else:
                    data = hv_send.at[phase, i, c * part_rows:(c + 1) * part_rows]
                    target = {"ctx": target_chip * 2 + c}
                mine = step * 2 + core
                for copy in (
                    remote(data, hv_recv.at[phase, i, core], hv_send_sem.at[phase, index], hv_recv_sem.at[phase, mine], target),
                    remote(stats, lse_recv.at[phase, i, core], lse_send_sem.at[phase, index], lse_recv_sem.at[phase, mine], target),
                ):
                    copy.start()
                    sent.append(copy)

    def combine(phase):
        local[2 * phase].wait()
        local[2 * phase + 1].wait()
        for i, step in enumerate(order):
            source_chip = peer_chip(chip, step, chips)
            for c in [other] if step == 0 else [0, 1]:
                index = step * 2 + c
                src = {"ctx": source_chip * 2 + c}
                remote(hv_send.at[phase, 0, :part_rows], hv_recv.at[phase, i, c], hv_send_sem.at[phase, 0], hv_recv_sem.at[phase, index], src).wait_recv()
                remote(lse_send.at[phase, 0], lse_recv.at[phase, i, c], lse_send_sem.at[phase, 0], lse_recv_sem.at[phase, index], src).wait_recv()
        for c in range(2):
            found = []
            for i in range(chips):
                mix[i] = lse_recv[phase, i, c].T
                first = pl.multiple_of((i % 2) * pair + core * part_rows, part_rows)
                found.append(mix[i, pl.ds(first, part_rows), :])
            top = functools.reduce(jnp.maximum, found)
            shares = [jnp.exp2(f - top) for f in found]
            whole = functools.reduce(jnp.add, shares)
            share = [f / whole for f in shares]
            for h in range(half):
                cols = slice(h * VDIM, (h + 1) * VDIM)
                total = jnp.zeros((part_rows, VDIM), jnp.float32)
                for i in range(chips):
                    total = total + hv_recv[phase, i, c, :, cols].astype(jnp.float32) * share[i][:, h:h + 1]
                first = (c * half + h) * VDIM
                hv[:, first:first + VDIM] = total.astype(jnp.bfloat16)

    piece = math.gcd(columns, 896)

    def project(dest):
        for b in range(columns // piece):
            cols = slice(b * piece, (b + 1) * piece)
            part[:, cols] = jnp.dot(hv[...], wo[dest, :, cols], preferred_element_type=jnp.float32)

    last = heads_axis - 1

    def chain(phase, dest, buffer, sends, recvs, target):
        return remote(parts_sent.at[phase, dest], buffer.at[phase, dest], sends.at[phase, dest], recvs.at[phase, dest], {"head": target})

    def down_copy(phase, dest):
        return chain(phase, dest, down, down_send, down_recv, row + 1)

    def up_copy(phase, dest):
        return chain(phase, dest, up, up_send, up_recv, row - 1)

    def down_wait(phase, dest):
        chain(phase, dest, down, down_send, down_recv, row - 1).wait_recv()

    def up_wait(phase, dest):
        chain(phase, dest, up, up_send, up_recv, row + 1).wait_recv()

    at_end = row // last
    upper = (2 * row) // heads_axis

    for phase in range(2):
        combine(phase)
        if phase == 0:
            for copy in weight_copies:
                copy.wait()

        def make_part(i, carry):
            dest = last - i + at_end * (2 * i - last)
            project(dest)
            parts_sent[phase, dest] = part[...].astype(jnp.bfloat16)

            @pl.when((row == 0) & (dest > 0))
            def _():
                down_copy(phase, dest).start()

            @pl.when((row == last) & (dest < last))
            def _():
                up_copy(phase, dest).start()

            return carry

        lax.fori_loop(0, heads_axis, make_part, 0)

        for i in range(heads_axis):
            turn = last - i // 2 if i % 2 == 0 else i // 2
            dest = turn + upper * (last - 2 * turn)

            @pl.when((row < dest) & (row > 0))
            def _():
                down_wait(phase, dest)
                parts_sent[phase, dest] = parts_sent[phase, dest] + down[phase, dest]
                down_copy(phase, dest).start()

            @pl.when((row > dest) & (row < last))
            def _():
                up_wait(phase, dest)
                parts_sent[phase, dest] = parts_sent[phase, dest] + up[phase, dest]
                up_copy(phase, dest).start()

    for phase in range(2):
        part[...] = parts_sent[phase, row].astype(jnp.float32)

        @pl.when(row > 0)
        def _():
            down_wait(phase, row)
            part[...] = part[...] + down[phase, row].astype(jnp.float32)

        @pl.when(row < last)
        def _():
            up_wait(phase, row)
            part[...] = part[...] + up[phase, row].astype(jnp.float32)

        out_ref[phase * part_rows:(phase + 1) * part_rows, :] = part[...].astype(jnp.bfloat16)

    for phase in range(2):
        for dest in range(heads_axis):
            @pl.when(row < dest)
            def _():
                down_copy(phase, dest).wait_send()

            @pl.when(row > dest)
            def _():
                up_copy(phase, dest).wait_send()

    cache_out.wait_send()
    for copy in sent:
        copy.wait_send()


def on_device(devices, heads_axis, q_nope, q_rope, w_uk, w_uv, w_o, latent_cache, group_start):
    tokens = q_nope.shape[0]
    half = w_uk.shape[0] // 2
    slots = latent_cache.shape[1]
    width = latent_cache.shape[0]
    columns = w_o.shape[1] // heads_axis
    chips = devices // 2
    part_rows = tokens // 2
    pair = 2 * part_rows
    lanes_total = devices * part_rows
    span = 2 * slots
    stat_rows = max(8, half)
    bf16, f32 = jnp.bfloat16, jnp.float32
    dma = pltpu.SemaphoreType.DMA
    any_space = pl.BlockSpec(memory_space=pl.ANY)
    return pl.pallas_call(
        functools.partial(kernel, devices, heads_axis, tokens, half, slots, columns),
        out_shape=jax.ShapeDtypeStruct((tokens, columns), bf16),
        in_specs=[pl.BlockSpec(memory_space=pltpu.SMEM)] + [any_space] * 6,
        out_specs=pl.BlockSpec(memory_space=pltpu.VMEM),
        scratch_shapes=[
            pltpu.VMEM((heads_axis, w_o.shape[0], columns), bf16),
            pltpu.VMEM((half, span, 2 * NOPE), bf16),
            pltpu.VMEM((half * VDIM, span), bf16),
            pltpu.VMEM((2, width, slots), bf16),
            pltpu.VMEM((half, NOPE, LATENT), bf16),
            pltpu.VMEM((half, LATENT, VDIM), bf16),
            pltpu.VMEM((devices, tokens, half * NOPE), bf16),
            pltpu.VMEM((devices, tokens, half * ROPE), bf16),
            pltpu.VMEM((2, span, lanes_total), f32),
            pltpu.VMEM((2, span, lanes_total), bf16),
            pltpu.VMEM((span, lanes_total), f32),
            pltpu.VMEM((2, chips, pair, half * VDIM), bf16),
            pltpu.VMEM((2, chips, 2, part_rows, half * VDIM), bf16),
            pltpu.VMEM((2, chips // 2, stat_rows, 2 * pair), f32),
            pltpu.VMEM((2, chips, 2, stat_rows, 2 * pair), f32),
            pltpu.VMEM((chips, 2 * pair, stat_rows), f32),
            pltpu.VMEM((part_rows, 2 * half * VDIM), bf16),
            pltpu.VMEM((part_rows, columns), f32),
            pltpu.VMEM((2, heads_axis, part_rows, columns), bf16),
            pltpu.VMEM((2, heads_axis, part_rows, columns), bf16),
            pltpu.VMEM((2, heads_axis, part_rows, columns), bf16),
            dma((11,)),
            dma((heads_axis,)),
            dma((2,)),
            dma((2, devices, 2)),
            dma((2, devices, 2)),
            dma((2, devices)),
            dma((2, devices)),
            dma((2, devices)),
            dma((2, devices)),
            dma((2, heads_axis)),
            dma((2, heads_axis)),
            dma((2, heads_axis)),
            dma((2, heads_axis)),
        ],
        compiler_params=pltpu.CompilerParams(
            collective_id=0, has_side_effects=True, vmem_limit_bytes=67043328
        ),
    )(group_start, q_nope, q_rope, w_uk, w_uv, w_o, latent_cache)


def solution(mesh):
    placed = (
        P("ctx", "head"),
        P("ctx", "head"),
        P("head", None, None),
        P("head", None, None),
        P("head", None),
        P(None, "ctx"),
        P(),
    )
    return jax.shard_map(
        functools.partial(on_device, mesh.shape["ctx"], mesh.shape["head"]),
        mesh=mesh, in_specs=placed, out_specs=P("ctx", "head"), check_vma=False,
    )
```
